32 devices in a mesh: groups: 2 (over x), psg: 16 (over z, y, core).
Axes of the slice: x: 2, y: 2, z: 4, core: 2. Of those that a mesh axis runs over, the one named last changes fastest.
Arguments:
- queries: bfloat16 [64, 32, 128], P(('groups', 'psg')), parts along dimension 0, may hold values from -0.29882812 to 0.29882812
- candidates: int32 [64, 512], P(('groups', 'psg')), parts along dimension 0, may hold values from 0 to 159
- centroids: bfloat16 [8192, 128], P('psg'), may hold values from -6 to 6
- bucket_weights: float32 [4, 128], replicated, may hold values from -1 to 1
- centroid_shard: int32 [32768, 1], P('psg'), may hold values from 0 to 15; in each aligned block of 2048 rows (0 to 2047, 2048 to 4095, ...) at most 256 rows name the same one
- centroid_row: int32 [32768], P('psg'), may hold values from 0 to 511
- residual_codes: int32 [32768, 128], P('psg'), may hold values from 0 to 3
- tile_count: int32 [160], replicated, may hold values from 1 to 3, 256 in all
- last_fill: int32 [160], replicated, may hold values from 1 to 128
Outputs:
- scores: float32 [64, 512], P(('groups', 'psg')), parts along dimension 0
The draws below stay inside these ranges and needn't reach their ends.
There are 2 independent parts, one for each index of `groups`. The reference program is written for one: setup_inputs(seed, part) draws one part's arguments, and reference() takes and returns one part's arrays. A program takes and returns all parts, laid end to end along the dimension named above; an argument that names none is the same for every part. Nothing has to cross between parts.
Inputs may be any that keep to these rules, and one draw needn't show every extreme that they name: `tile_count`: tiles are numbered along psg, device k holding tiles k * 16 onward; the counts sum to 256, so a passage may continue on the next device. `centroid_shard`: among the 2048 token slots of one device, at most 256 name the same device; on some device some value is named exactly 256 times.
All inputs are finite; a program needn't handle non-finite values.
Results may differ from the reference program's by a relative error of at most 0.0003.
Values may be sent and summed in bfloat16 or wider, within the bound.
No kernel may reach another device: no remote copies, remote signals or barrier semaphores. Data moves between devices by JAX's collectives and lax.ppermute only.
A program may use at most 64 MiB of HBM per device.

```python
import math
import jax
import jax.numpy as jnp
import numpy as np
from jax import lax

DIM = 128
QTOK = 32
TILE = 128
MAXT = 3
CENT_DEV = 512
TILES_DEV = 16
NCAND = 512
CAP = 256
QUERIES = 32
NT = 256
NP = 160
NCENT = 8192
TOKENS_ALL = 32768
N_PSG = 16


def with_ends(values, own_key, low, high):
    extent = values.shape
    spot = [jax.random.randint(jax.random.fold_in(own_key, axis), (), 0, extent[axis]) for axis in range(len(extent))]
    values = values.at[tuple(spot)].set(low)
    longest = extent.index(max(extent))
    spot[longest] = (spot[longest] + 1) % extent[longest]
    return values.at[tuple(spot)].set(high)


def shard_levels(rng, shape, cuts, least, top_value):
    def one(dim, parts):
        draws = jax.random.uniform(jax.random.fold_in(jax.random.fold_in(rng, 6), dim), (parts,), jnp.float32, least / len(cuts), top_value / len(cuts))
        return jnp.repeat(jnp.exp(draws), shape[dim] // parts).reshape((-1,) + (1,) * (len(shape) - dim - 1))

    loudness = one(*cuts[0])
    for cut in cuts[1:]:
        loudness = loudness * one(*cut)
    return loudness


def length_profile(number_of, total, bound, slope):
    weights = [(1 << 20) // math.isqrt(grade ** slope) + 1 for grade in range(2, number_of + 1)]
    surplus, holding = total - bound - (number_of - 1), [1] * (number_of - 1)
    while surplus > 0:
        movable = [i for i in range(number_of - 1) if holding[i] < bound]
        mass, budget = sum([weights[i] for i in movable]), surplus
        for i in movable:
            addition = min(bound - holding[i], max(1, budget * weights[i] // mass), surplus)
            holding[i] = holding[i] + addition
            surplus = surplus - addition
    return np.array([bound] + holding)


def ragged_sizes(rng, count, total, bound, slope):
    if count == 2:
        one = jax.random.randint(rng, (), max(1, total - bound), min(bound, total - 1) + 1)
        return jnp.stack([one, total - one])
    lengths = jnp.asarray(length_profile(count, total, bound, slope), jnp.int32)
    twos = (count - 1) // 2
    giver, taker = lengths[1:1 + 2 * twos:2], lengths[2:2 + 2 * twos:2]
    margin = jnp.minimum(giver - 1, bound - taker)
    passed = jax.random.randint(jax.random.fold_in(rng, 1), (twos,), 0, 1 << 20) % (margin + 1)
    lengths = lengths.at[1:1 + 2 * twos:2].set(giver - passed).at[2:2 + 2 * twos:2].set(taker + passed)
    return lengths[jax.random.permutation(jax.random.fold_in(rng, 2), count)]


def routed_block(rng, own, number, rows, count, top, reach, skew):
    ranking = jax.random.permutation(rng, count)
    crowded, common = load_shares(count, rows * top, reach, skew, True), load_shares(count, rows * top, reach, skew, False)
    places = jnp.arange(count)

    def named(sizes, rotation):
        used = int((sizes > 0).sum())
        fixed = max(1, used // 4)
        moved = fixed + (places - fixed + rotation * (used - fixed)) % max(1, count - fixed)
        return jnp.zeros((count,), jnp.int32).at[ranking[jnp.where(places < fixed, places, moved)]].set(jnp.asarray(sizes, jnp.int32))

    sizes = jnp.where(number % 4 == 0, named(crowded, number // 4), named(common, number - number // 4 - 1))
    mixed = jax.random.permutation(jax.random.fold_in(own, 3), count)
    donor, receiver = mixed[0:count // 2 * 2:2], mixed[1:count // 2 * 2:2]
    slack = jnp.minimum(sizes[donor] - 1, reach - sizes[receiver]) // 2
    slack = jnp.where((donor == ranking[0]) | (receiver == ranking[0]) | (sizes[receiver] == 0), 0, jnp.maximum(slack, 0))
    moved = jax.random.randint(jax.random.fold_in(own, 4), (count // 2,), 0, 1 << 20) % (slack + 1)
    sizes = sizes.at[donor].add(-moved).at[receiver].add(moved)
    items = jnp.searchsorted(jnp.cumsum(sizes), jnp.arange(rows * top), side="right").astype(jnp.int32)
    listing = items.reshape(top, rows).T
    listing = listing[jax.random.permutation(jax.random.fold_in(own, 1), rows)]
    rotation = jax.random.randint(jax.random.fold_in(own, 2), (rows, 1), 0, top)
    return jnp.take_along_axis(listing, (jnp.arange(top)[None, :] + rotation) % top, axis=1)


def load_shares(count, total, most, skew, full):
    loads = [(1 << 20) // math.isqrt(rank ** skew) + 1 for rank in range(1, count + 1)]
    largest = most if full else min(most, max(-(-total // count), total * loads[0] // sum(loads)))
    least = 1 if total - largest >= count - 1 else 0
    given, surplus = [largest] + [least] * (count - 1), total - largest - least * (count - 1)
    while surplus > 0:
        movable = [i for i in range(1, count) if given[i] < largest] or [i for i in range(1, count) if given[i] < most]
        pool, budget = sum([loads[i] for i in movable]), surplus
        for i in movable:
            more = min(most - given[i], max(1, budget * loads[i] // pool), surplus)
            given[i] = given[i] + more
            surplus = surplus - more
    return np.array(given)


def gaussian(rng, shape, width, most, split=(), kind=jnp.bfloat16):
    factor_of = shard_levels(rng, shape, split, -0.22, 0.18) if split else 1.0
    result = jax.random.normal(rng, shape, jnp.float32) * width * factor_of
    return jnp.minimum(jnp.maximum(result, -most), most).astype(kind)


def setup_inputs(seed: int = 0, part: int = 0) -> dict:
    keys = jax.random.split(jax.random.key(seed), 10)
    part_keys = jax.random.split(jax.random.fold_in(keys[9], part), 10)
    queries = gaussian(part_keys[0], (QUERIES, QTOK, DIM), 0.05, 0.29882812, ((0, 16),))
    candidates = with_ends(jax.random.randint(part_keys[1], (QUERIES, NCAND), 0, NP), jax.random.fold_in(part_keys[1], 1), 0, NP - 1).astype(jnp.int32)
    centroids = gaussian(keys[2], (NCENT, DIM), 1.0, 6.0, ((0, 16),))
    bucket_weights = jnp.clip(jax.random.uniform(keys[3], (4, DIM), jnp.float32, -1.0, 1.0), -1.0, 1.0)
    centroid_shard_keys = jax.random.split(jax.random.fold_in(keys[4], 1), TOKENS_ALL // (TILES_DEV * TILE))
    centroid_shard_turns = jax.random.permutation(jax.random.fold_in(keys[4], 3), TOKENS_ALL // (TILES_DEV * TILE))
    centroid_shard = jax.vmap(lambda own, number: routed_block(jax.random.fold_in(keys[4], 2), own, number, TILES_DEV * TILE, N_PSG, 1, CAP, 1))(centroid_shard_keys, centroid_shard_turns).reshape((TOKENS_ALL, 1))
    centroid_row = with_ends(jax.random.randint(keys[5], (TOKENS_ALL,), 0, CENT_DEV), jax.random.fold_in(keys[5], 1), 0, CENT_DEV - 1).astype(jnp.int32)
    residual_codes = with_ends(jax.random.randint(keys[6], (TOKENS_ALL, DIM), 0, 4), jax.random.fold_in(keys[6], 1), 0, 3).astype(jnp.int32)
    tile_count = ragged_sizes(keys[7], NP, NT, MAXT, 1).astype(jnp.int32)
    last_fill = with_ends(jax.random.randint(keys[8], (NP,), 1, TILE + 1), jax.random.fold_in(keys[8], 1), 1, TILE).astype(jnp.int32)
    return dict(queries=queries, candidates=candidates, centroids=centroids, bucket_weights=bucket_weights, centroid_shard=centroid_shard, centroid_row=centroid_row, residual_codes=residual_codes, tile_count=tile_count, last_fill=last_fill)


epsilon = 1e-06

def tile_layout(tile_count, last_fill, total_tiles, tile_len):
    starts = (jnp.cumsum(tile_count) - tile_count).astype(jnp.int32)
    last_tile = (starts + tile_count - 1).astype(jnp.int32)
    tile_fill = jnp.full((total_tiles,), tile_len, jnp.int32).at[last_tile].set(last_fill.astype(jnp.int32))
    return (starts, tile_fill)

def decode(picked, residual_codes, bucket_weights):
    residual = jnp.zeros(residual_codes.shape, jnp.float32)
    for bucket in range(4):
        residual = residual + jnp.where(residual_codes == bucket, bucket_weights[bucket][None, :], jnp.float32(0.0))
    summed = picked.astype(jnp.float32) + residual
    scale = lax.rsqrt(lax.optimization_barrier(jnp.sum(summed * summed, axis=1, keepdims=True)) + epsilon)
    return (summed * scale).astype(jnp.bfloat16)

def assemble(own_maxima, candidates, starts, tile_count, query_len):
    num_queries, num_cand = candidates.shape
    own_maxima = own_maxima.reshape(num_queries, query_len, -1)
    tile_steps = jnp.arange(MAXT, dtype=jnp.int32)
    tile_index = starts[candidates][..., None] + tile_steps
    live_mask = tile_steps < tile_count[candidates][..., None]
    tile_index = jnp.where(live_mask, tile_index, 0).astype(jnp.int32)
    values = jax.vmap(lambda matrix, indices: matrix[:, indices.reshape(-1)])(own_maxima, tile_index)
    values = values.reshape(num_queries, query_len, num_cand, MAXT)
    values = jnp.where(live_mask[:, None], values, -jnp.inf)
    return lax.optimization_barrier(jnp.sum(lax.optimization_barrier(jnp.max(values, axis=3)), axis=1))

def reference(queries, candidates, centroids, bucket_weights, centroid_shard, centroid_row, residual_codes, tile_count, last_fill):
    total_tiles = TILES_DEV * N_PSG
    starts, tile_fill = tile_layout(tile_count, last_fill, total_tiles, TILE)
    codes = (centroid_shard[:, 0] * CENT_DEV + centroid_row).astype(jnp.int32)
    picked = jnp.take(centroids, codes, axis=0)
    embedded = decode(picked, residual_codes, bucket_weights)
    token_mask = jnp.arange(TILE, dtype=jnp.int32)[None, :] < tile_fill[:, None]
    pad_bias = jnp.where(token_mask, jnp.float32(0.0), -jnp.inf).reshape(N_PSG, TILES_DEV * TILE)
    key_blocks = embedded.reshape(N_PSG, TILES_DEV * TILE, DIM)
    flat_rows = queries.reshape(-1, DIM)

    def one_block(inputs):
        key_block, bias_block = inputs
        block_scores = jnp.dot(flat_rows, key_block.T, preferred_element_type=jnp.float32) + bias_block[None, :]
        return lax.optimization_barrier(jnp.max(block_scores.reshape(flat_rows.shape[0], TILES_DEV, TILE), axis=2))
    maxima = lax.map(one_block, (key_blocks, pad_bias))
    maxima = jnp.transpose(maxima, (1, 0, 2)).reshape(flat_rows.shape[0], total_tiles)
    return assemble(maxima, candidates, starts, tile_count, QTOK)
```

```python
import functools

import jax
import jax.numpy as jnp
from jax import lax
from jax.experimental import pallas as pl
from jax.experimental.pallas import tpu as pltpu
from jax.sharding import PartitionSpec as P

TILE = 128
LANES = 128
EPSILON = 1e-06


def swap(x, offset):
    n = lax.axis_size("psg")
    return lax.ppermute(x, "psg", [(i, i ^ offset) for i in range(n)])


def spread(own):
    n = lax.axis_size("psg")
    bits = [1 << k for k in range(n.bit_length() - 1)]
    held = [((0,), own)]
    stages = []
    rest = bits[:0:-1]
    while rest:
        size = 1 if not stages else min(2, len(rest))
        stages.append(rest[:size])
        rest = rest[size:]
    stages.append(bits[:1])
    for stage in stages:
        offsets = [0]
        for bit in stage:
            offsets += [o ^ bit for o in offsets]
        if len(held) > 8:
            held = [(sum([o for o, _ in held], ()), jnp.concatenate([a for _, a in held]))]
        held = held + [
            (tuple(o ^ offset for o in names), swap(array, offset))
            for names, array in held
            for offset in offsets[1:]
        ]
    return held


def layout_kernel(tile_len, count_ref, last_ref, start_ref, fill_ref, more_ref):
    most = fill_ref.shape[0]

    def clear(t, carry):
        fill_ref[t] = tile_len
        more_ref[t] = 0
        return carry

    def passage(p, start):
        count = count_ref[p]
        start_ref[p] = start
        more_ref[start] = count - 1
        fill_ref[start] = tile_len
        more_ref[start + 1] = count - 2
        fill_ref[start + 1] = tile_len
        more_ref[start + 2] = 0
        fill_ref[start + 2] = tile_len
        fill_ref[start + count - 1] = last_ref[p]
        return start + count

    total = lax.fori_loop(0, count_ref.shape[0], passage, jnp.int32(0))
    lax.fori_loop(total, most, clear, 0)

    def pad(p, carry):
        start_ref[p] = 0
        return carry

    lax.fori_loop(count_ref.shape[0], start_ref.shape[0], pad, 0)


def tile_layout(tile_count, last_fill, total_tiles):
    passages = -(-tile_count.shape[0] // LANES) * LANES
    smem = pl.BlockSpec(memory_space=pltpu.SMEM)
    room = total_tiles + LANES
    return pl.pallas_call(
        functools.partial(layout_kernel, TILE),
        out_shape=(
            jax.ShapeDtypeStruct((passages,), jnp.int32),
            jax.ShapeDtypeStruct((room,), jnp.int32),
            jax.ShapeDtypeStruct((room,), jnp.int32),
        ),
        in_specs=[smem, smem],
        out_specs=(smem, smem, smem),
        name="tile_layout",
    )(tile_count, last_fill)


def maxima_kernel(names, cent_dev, query_rows, place_ref, code_ref, fill_ref, residual_ref, weight_ref, *rest):
    pieces = rest[: len(names)]
    out_ref, book_ref, query_ref, picked_ref, embedded_ref = rest[len(names) :]
    index = place_ref[0]
    each = cent_dev + query_rows
    for offsets, piece in zip(names, pieces):
        for k, offset in enumerate(offsets):
            source = index ^ offset
            book_at = pl.multiple_of(source * cent_dev, cent_dev)
            book_ref[pl.ds(book_at, cent_dev), :] = piece[k * each : k * each + cent_dev, :].astype(jnp.float32)
            query_at = pl.multiple_of(source * query_rows, query_rows)
            query_ref[pl.ds(query_at, query_rows), :] = piece[k * each + cent_dev : (k + 1) * each, :]

    tokens = residual_ref.shape[0]
    unroll = 16

    def pick(step, carry):
        base = pl.multiple_of(step * unroll, unroll)
        for u in range(unroll):
            picked_ref[pl.ds(base + u, 1), :] = book_ref[pl.ds(code_ref[base + u], 1), :]
        return carry

    lax.fori_loop(0, tokens // unroll, pick, 0)

    tiles = tokens // TILE
    slot = lax.broadcasted_iota(jnp.int32, (TILE, 1), 0)
    weights = [weight_ref[b : b + 1, :] for b in range(4)]

    def decode(t, carry):
        rows = pl.ds(pl.multiple_of(t * TILE, TILE), TILE)
        codes = residual_ref[rows, :]
        residual = jnp.where(
            codes < 2,
            jnp.where(codes == 0, weights[0], weights[1]),
            jnp.where(codes == 2, weights[2], weights[3]),
        )
        summed = picked_ref[rows, :] + residual
        scale = lax.rsqrt(jnp.sum(summed * summed, axis=1, keepdims=True) + EPSILON)
        embedded = summed * scale
        fill = fill_ref[index * tiles + t]
        embedded = jnp.where(slot < fill, embedded, embedded[0:1, :])
        embedded_ref[rows, :] = embedded.astype(jnp.bfloat16)
        return carry

    lax.fori_loop(0, tiles, decode, 0)

    width = 2 * LANES
    per = LANES // query_rows
    deep = tiles // per
    lane = lax.broadcasted_iota(jnp.int32, (deep, LANES), 1)

    def score(step, carry):
        q = query_ref[pl.ds(pl.multiple_of(step * width, width), width), :]
        rows = []
        for t in range(tiles):
            products = lax.dot_general(
                embedded_ref[t * TILE : (t + 1) * TILE, :],
                q,
                (((1,), (1,)), ((), ())),
                preferred_element_type=jnp.float32,
            )
            rows.append(jnp.max(products, axis=0, keepdims=True))
        best = jnp.concatenate(rows, axis=0)
        for b in range(width // LANES):
            block = best[:, b * LANES : (b + 1) * LANES]
            for peer in range(per):
                made = None
                for g in range(per):
                    part = block[g * deep : (g + 1) * deep, :]
                    turn = (g - peer) * query_rows % LANES
                    if turn:
                        part = pltpu.roll(part, turn, 1)
                    made = part if made is None else jnp.where(lane < g * query_rows, made, part)
                out_ref[step * (width // query_rows) + b * per + peer] = made
        return carry

    lax.fori_loop(0, query_ref.shape[0] // width, score, 0)


def tile_maxima(held, index, codes, fill, residual_codes, bucket_weights, cent_dev, query_rows):
    n = lax.axis_size("psg")
    tokens, dim = residual_codes.shape
    per = LANES // query_rows
    smem = pl.BlockSpec(memory_space=pltpu.SMEM)
    vmem = pl.BlockSpec(memory_space=pltpu.VMEM)
    names = tuple(o for o, _ in held)
    return pl.pallas_call(
        functools.partial(maxima_kernel, names, cent_dev, query_rows),
        out_shape=jax.ShapeDtypeStruct((n, tokens // TILE // per, LANES), jnp.float32),
        in_specs=[smem, smem, smem, vmem, vmem] + [vmem] * len(held),
        out_specs=vmem,
        scratch_shapes=[
            pltpu.VMEM((n * cent_dev, dim), jnp.float32),
            pltpu.VMEM((n * query_rows, dim), jnp.bfloat16),
            pltpu.VMEM((tokens, dim), jnp.float32),
            pltpu.VMEM((tokens, dim), jnp.bfloat16),
        ],
        name="tile_maxima",
    )(index, codes, fill, residual_codes, bucket_weights, *[a for _, a in held])


def lookup(table, rows_of):
    within = rows_of & (LANES - 1)
    block = rows_of >> 7
    found = None
    for b, values in enumerate(table):
        got = jnp.take_along_axis(values, within, axis=1, mode="promise_in_bounds")
        found = got if found is None else jnp.where(block == b, got, found)
    return found


def assemble_kernel(query_len, maxima_ref, more_ref, start_ref, candidate_ref, out_ref, tiles_ref):
    n, deep, _ = maxima_ref.shape
    queries, candidates = candidate_ref.shape
    query_rows = queries * query_len
    per = LANES // query_rows
    total = n * deep * per
    for j in range(n):
        got = maxima_ref[j]
        for g in range(per):
            at = (j * per + g) * deep
            part = got if g == 0 else pltpu.roll(got, LANES - g * query_rows, 1)
            tiles_ref[at : at + deep, :] = part
    tiles_ref[total : total + 8, :] = jnp.zeros((8, LANES), jnp.float32)
    more = more_ref[...]
    combined = tiles_ref[0:total, :]
    combined = jnp.maximum(combined, jnp.where(more >= 1, tiles_ref[1 : total + 1, :], combined))
    combined = jnp.maximum(combined, jnp.where(more >= 2, tiles_ref[2 : total + 2, :], combined))
    chunks = candidates // LANES
    row = lax.broadcasted_iota(jnp.int32, (8, LANES), 0)
    lane = lax.broadcasted_iota(jnp.int32, (8, LANES), 1)
    high = combined.astype(jnp.bfloat16)
    left = combined - high.astype(jnp.float32)
    middle = left.astype(jnp.bfloat16)
    low = (left - middle.astype(jnp.float32)).astype(jnp.bfloat16)
    groups = [(q, c) for q in range(queries) for c in range(chunks)]
    for first in range(0, len(groups), 8):
        some = groups[first : first + 8]
        owner = jnp.zeros((8, LANES), jnp.int32)
        wanted = jnp.zeros((8, LANES), jnp.int32)
        for r, (q, c) in enumerate(some):
            owner = jnp.where(row == r, q, owner)
            ids = candidate_ref[q : q + 1, c * LANES : (c + 1) * LANES]
            wanted = jnp.where(row == r, ids, wanted)
        select = jnp.where((lane >= owner * query_len) & (lane < (owner + 1) * query_len), 1.0, 0.0).astype(jnp.bfloat16)
        sums = None
        for part in (low, middle, high):
            term = lax.dot_general(select, part, (((1,), (1,)), ((), ())), preferred_element_type=jnp.float32)
            sums = term if sums is None else sums + term
        starts = [
            jnp.broadcast_to(start_ref[b : b + 1, :], (8, LANES)) for b in range(start_ref.shape[0])
        ]
        first_tile = lookup(starts, wanted)
        found = lookup([sums[:, b * LANES : (b + 1) * LANES] for b in range(-(-total // LANES))], first_tile)
        for r, (q, c) in enumerate(some):
            out_ref[q : q + 1, c * LANES : (c + 1) * LANES] = found[r : r + 1, :]


def assemble(own_maxima, more, starts, candidates, query_len):
    n, deep, _ = own_maxima.shape
    per = LANES // (candidates.shape[0] * query_len)
    total = n * deep * per
    vmem = pl.BlockSpec(memory_space=pltpu.VMEM)
    return pl.pallas_call(
        functools.partial(assemble_kernel, query_len),
        out_shape=jax.ShapeDtypeStruct(candidates.shape, jnp.float32),
        in_specs=[vmem] * 4,
        out_specs=vmem,
        scratch_shapes=[pltpu.VMEM((total + 8, LANES), jnp.float32)],
        name="assemble",
    )(own_maxima, jnp.broadcast_to(more[:total, None], (total, LANES)), starts.reshape(-1, LANES), candidates)


def per_device(
    queries,
    candidates,
    centroids,
    bucket_weights,
    centroid_shard,
    centroid_row,
    residual_codes,
    tile_count,
    last_fill,
):
    n = lax.axis_size("psg")
    index = lax.axis_index("psg").astype(jnp.int32)
    cent_dev = centroids.shape[0]
    num_queries, query_len, dim = queries.shape
    query_rows = num_queries * query_len
    total_tiles = residual_codes.shape[0] // TILE * n
    held = spread(jnp.concatenate([centroids, queries.reshape(query_rows, dim)]))
    codes = centroid_shard[:, 0] * cent_dev + centroid_row
    starts, fill, more = tile_layout(tile_count, last_fill, total_tiles)
    maxima = tile_maxima(
        held, index.reshape(1), codes, fill, residual_codes, bucket_weights, cent_dev, query_rows
    )
    own_maxima = lax.all_to_all(maxima, "psg", split_axis=0, concat_axis=0, tiled=True)
    return assemble(own_maxima, more, starts, candidates, query_len)


def solution(mesh):
    placed = (
        P(("groups", "psg"), None, None),
        P(("groups", "psg"), None),
        P("psg", None),
        P(),
        P("psg", None),
        P("psg"),
        P("psg", None),
        P(),
        P(),
    )
    return jax.shard_map(
        per_device,
        mesh=mesh,
        in_specs=placed,
        out_specs=P(("groups", "psg"), None),
        check_vma=False,
    )
```

```python
import functools

import jax
import jax.numpy as jnp
from jax import lax
from jax.experimental import pallas as pl
from jax.experimental.pallas import tpu as pltpu
from jax.sharding import PartitionSpec as P


TILE = 128
LANES = 128
EPSILON = 1e-06
GRANT = 8 << 20


def swap(x, offset):
    n = lax.axis_size("psg")
    return lax.ppermute(x, "psg", [(i, i ^ offset) for i in range(n)])


def bits_of(n):
    return [1 << k for k in reversed(range(n.bit_length() - 1))]


def spread(own, beside):
    bits = bits_of(lax.axis_size("psg"))
    far, mid, low = bits[0], bits[1], bits[2]
    held = {0: own}
    held[far] = swap(own, far)
    held[low] = swap(own, low)
    held[mid ^ low] = swap(own, mid ^ low)
    held[mid] = swap(own, mid)
    held[far ^ low] = swap(held[far], low)
    held[far ^ mid ^ low] = swap(held[far], mid ^ low)
    held[far ^ mid] = swap(held[far], mid)
    held[far ^ low], beside = lax.optimization_barrier((held[far ^ low], beside))
    pieces = [((o,), array) for o, array in held.items()]
    for bit in bits[3:]:
        if len(pieces) > 8:
            pieces = [(sum([o for o, _ in pieces], ()), jnp.concatenate([a for _, a in pieces]))]
        pieces = pieces + [(tuple(o ^ bit for o in names), swap(array, bit)) for names, array in pieces]
    return pieces, beside


def passages(count_ref):
    count = count_ref[...]
    before = lax.broadcasted_iota(jnp.int32, (LANES, LANES), 0) < lax.broadcasted_iota(jnp.int32, (LANES, LANES), 1)
    within = jnp.dot(
        count.astype(jnp.float32).astype(jnp.bfloat16),
        jnp.where(before, 1.0, 0.0).astype(jnp.bfloat16),
        preferred_element_type=jnp.float32,
    ).astype(jnp.int32)
    sums = jnp.sum(count, axis=1, keepdims=True)
    passed = jnp.zeros((1, 1), jnp.int32)
    spans = []
    for b in range(count.shape[0]):
        held = count[b : b + 1, :]
        start = within[b : b + 1, :] + passed
        passed = passed + sums[b : b + 1, :]
        spans.append((start, jnp.where(held > 0, start + held - 1, -1)))
    return spans


def fill_kernel(place_ref, count_ref, last_ref, fill_ref):
    rows = fill_ref.shape[0]
    tile = lax.broadcasted_iota(jnp.int32, (rows, LANES), 0) + place_ref[0] * rows
    total = jnp.zeros((rows, LANES), jnp.int32)
    for b, (_, last) in enumerate(passages(count_ref)):
        total = total + jnp.where(tile == last, last_ref[b : b + 1, :] - TILE, 0)
    fill_ref[...] = jnp.broadcast_to(jnp.sum(total, axis=1, keepdims=True), (rows, LANES)) + TILE


def start_kernel(count_ref, start_ref, more_ref):
    spans = passages(count_ref)
    for b, (start, _) in enumerate(spans):
        start_ref[b : b + 1, :] = start

    def chunk(step, carry):
        first = pl.multiple_of(step * LANES, LANES)
        tile = lax.broadcasted_iota(jnp.int32, (LANES, LANES), 0) + first
        total = jnp.zeros((LANES, LANES), jnp.int32)
        for start, last in spans:
            total = total + jnp.where((start <= tile) & (tile <= last), last - tile, 0)
        more_ref[pl.ds(first, LANES), :] = jnp.broadcast_to(jnp.sum(total, axis=1, keepdims=True), (LANES, LANES))
        return carry

    lax.fori_loop(0, more_ref.shape[0] // LANES, chunk, 0)


def in_blocks(values):
    blocks = -(-values.shape[0] // LANES)
    return jnp.pad(values, (0, blocks * LANES - values.shape[0])).reshape(blocks, LANES)


def own_fill(place, counts, lasts, tiles_dev):
    vmem = pl.BlockSpec(memory_space=pltpu.VMEM)
    return pl.pallas_call(
        fill_kernel,
        out_shape=jax.ShapeDtypeStruct((tiles_dev, LANES), jnp.int32),
        in_specs=[pl.BlockSpec(memory_space=pltpu.SMEM), vmem, vmem],
        out_specs=vmem,
        compiler_params=pltpu.CompilerParams(vmem_limit_bytes=GRANT),
        name="own_fill",
    )(place, counts, lasts)


def tile_starts(counts, total_tiles):
    vmem = pl.BlockSpec(memory_space=pltpu.VMEM)
    return pl.pallas_call(
        start_kernel,
        out_shape=(
            jax.ShapeDtypeStruct(counts.shape, jnp.int32),
            jax.ShapeDtypeStruct((-(-total_tiles // LANES) * LANES, LANES), jnp.int32),
        ),
        in_specs=[vmem],
        out_specs=(vmem, vmem),
        compiler_params=pltpu.CompilerParams(vmem_limit_bytes=GRANT),
        name="tile_starts",
    )(counts)


def maxima_kernel(names, query_rows, place_ref, code_ref, fill_ref, residual_ref, *rest):
    pieces = rest[: len(names)]
    out_ref, book_ref, query_ref, even_ref, odd_ref, embedded_ref = rest[len(names) :]
    index = place_ref[0]
    each = pieces[0].shape[0] // len(names[0])
    cent_dev = each - query_rows
    for offsets, piece in zip(names, pieces):
        for k, offset in enumerate(offsets):
            book_at = pl.multiple_of((index ^ offset) * cent_dev, cent_dev)
            query_at = pl.multiple_of((index ^ offset) * query_rows, query_rows)
            query_ref[pl.ds(query_at, query_rows), :] = piece[k * each + cent_dev : (k + 1) * each, :]

            def expand(step, carry, piece=piece, start=k * each, book_at=book_at):
                at = pl.multiple_of(step * LANES, LANES)
                rows = piece[pl.ds(start + at, LANES), :].astype(jnp.float32)
                book_ref[pl.ds(book_at + at, LANES), :] = rows
                return carry

            lax.fori_loop(0, cent_dev // LANES, expand, 0, unroll=len(names) > 8)

    tiles = residual_ref.shape[0] // TILE
    slot = lax.broadcasted_iota(jnp.int32, (TILE, LANES), 0)

    def pick(tile, into):
        base = tile * TILE
        for u in range(TILE):
            into[u : u + 1, :] = book_ref[pl.ds(code_ref[base + u], 1), :]

    def decode(tile, picked):
        rows = pl.ds(pl.multiple_of(tile * TILE, TILE), TILE)
        summed = picked[...] + residual_ref[rows, :]
        scale = lax.rsqrt(jnp.sum(summed * summed, axis=1, keepdims=True) + EPSILON)
        embedded = summed * scale
        embedded = jnp.where(slot < fill_ref[pl.ds(tile, 1), :], embedded, embedded[0:1, :])
        embedded_ref[rows, :] = embedded.astype(jnp.bfloat16)

    pick(0, even_ref)

    def pair(step, carry):
        tile = 2 * step
        pick(tile + 1, odd_ref)
        decode(tile, even_ref)
        pick(jnp.minimum(tile + 2, tiles - 1), even_ref)
        decode(tile + 1, odd_ref)
        return carry

    lax.fori_loop(0, tiles // 2, pair, 0)

    width = 2 * LANES
    per = LANES // query_rows
    deep = tiles // per
    lane = lax.broadcasted_iota(jnp.int32, (deep, LANES), 1)

    def score(step, carry):
        q = query_ref[pl.ds(pl.multiple_of(step * width, width), width), :]
        rows = []
        for t in range(tiles):
            products = lax.dot_general(
                embedded_ref[t * TILE : (t + 1) * TILE, :],
                q,
                (((1,), (1,)), ((), ())),
                preferred_element_type=jnp.float32,
            )
            rows.append(jnp.max(products, axis=0, keepdims=True))
        best = jnp.concatenate(rows, axis=0)
        for b in range(width // LANES):
            block = best[:, b * LANES : (b + 1) * LANES]
            for turn in range(per):
                made = None
                for g in range(per):
                    part = block[g * deep : (g + 1) * deep, :]
                    shift = (g - turn) * query_rows % LANES
                    if shift:
                        part = pltpu.roll(part, shift, 1)
                    made = part if made is None else jnp.where(lane < g * query_rows, made, part)
                out_ref[step * (width // query_rows) + b * per + turn] = made
        return carry

    lax.fori_loop(0, query_ref.shape[0] // width, score, 0)


def tile_maxima(held, place, codes, fill, residual, query_rows):
    n = lax.axis_size("psg")
    tokens, dim = residual.shape
    cent_dev = held[0][1].shape[0] // len(held[0][0]) - query_rows
    per = LANES // query_rows
    smem = pl.BlockSpec(memory_space=pltpu.SMEM)
    vmem = pl.BlockSpec(memory_space=pltpu.VMEM)
    names = tuple(o for o, _ in held)
    room = (n * (cent_dev * 6 + query_rows * 4) + tokens * 6) * dim + GRANT
    return pl.pallas_call(
        functools.partial(maxima_kernel, names, query_rows),
        out_shape=jax.ShapeDtypeStruct((n, tokens // TILE // per, LANES), jnp.float32),
        in_specs=[smem, smem, vmem, vmem] + [vmem] * len(held),
        out_specs=vmem,
        scratch_shapes=[
            pltpu.VMEM((n * cent_dev, dim), jnp.float32),
            pltpu.VMEM((n * query_rows, dim), jnp.bfloat16),
            pltpu.VMEM((TILE, dim), jnp.float32),
            pltpu.VMEM((TILE, dim), jnp.float32),
            pltpu.VMEM((tokens, dim), jnp.bfloat16),
        ],
        compiler_params=pltpu.CompilerParams(vmem_limit_bytes=room),
        name="tile_maxima",
    )(place, codes, fill, residual, *[a for _, a in held])


def lookup(table, rows_of):
    within = rows_of & (LANES - 1)
    block = rows_of >> 7
    found = None
    for b, values in enumerate(table):
        got = jnp.take_along_axis(values, within, axis=1, mode="promise_in_bounds")
        found = got if found is None else jnp.where(block == b, got, found)
    return found


def assemble_kernel(query_len, maxima_ref, more_ref, start_ref, candidate_ref, out_ref, tiles_ref):
    n, deep, _ = maxima_ref.shape
    queries, candidates = candidate_ref.shape
    query_rows = queries * query_len
    per = LANES // query_rows
    total = n * deep * per
    for j in range(n):
        got = maxima_ref[j]
        for g in range(per):
            at = (j * per + g) * deep
            part = got if g == 0 else pltpu.roll(got, LANES - g * query_rows, 1)
            tiles_ref[at : at + deep, :] = part
    tiles_ref[total : total + 8, :] = jnp.zeros((8, LANES), jnp.float32)
    more = more_ref[0:total, :]
    combined = tiles_ref[0:total, :]
    combined = jnp.maximum(combined, jnp.where(more >= 1, tiles_ref[1 : total + 1, :], combined))
    combined = jnp.maximum(combined, jnp.where(more >= 2, tiles_ref[2 : total + 2, :], combined))
    chunks = candidates // LANES
    row = lax.broadcasted_iota(jnp.int32, (8, LANES), 0)
    lane = lax.broadcasted_iota(jnp.int32, (8, LANES), 1)
    high = combined.astype(jnp.bfloat16)
    left = combined - high.astype(jnp.float32)
    middle = left.astype(jnp.bfloat16)
    low = (left - middle.astype(jnp.float32)).astype(jnp.bfloat16)
    groups = [(q, c) for q in range(queries) for c in range(chunks)]
    for first in range(0, len(groups), 8):
        some = groups[first : first + 8]
        owner = jnp.zeros((8, LANES), jnp.int32)
        wanted = jnp.zeros((8, LANES), jnp.int32)
        for r, (q, c) in enumerate(some):
            owner = jnp.where(row == r, q, owner)
            ids = candidate_ref[q : q + 1, c * LANES : (c + 1) * LANES]
            wanted = jnp.where(row == r, ids, wanted)
        select = jnp.where((lane >= owner * query_len) & (lane < (owner + 1) * query_len), 1.0, 0.0).astype(jnp.bfloat16)
        sums = None
        for part in (low, middle, high):
            term = lax.dot_general(select, part, (((1,), (1,)), ((), ())), preferred_element_type=jnp.float32)
            sums = term if sums is None else sums + term
        starts = [
            jnp.broadcast_to(start_ref[b : b + 1, :], (8, LANES)) for b in range(start_ref.shape[0])
        ]
        first_tile = lookup(starts, wanted)
        found = lookup([sums[:, b * LANES : (b + 1) * LANES] for b in range(-(-total // LANES))], first_tile)
        for r, (q, c) in enumerate(some):
            out_ref[q : q + 1, c * LANES : (c + 1) * LANES] = found[r : r + 1, :]


def assemble(own_maxima, more, starts, candidates, query_len):
    n, deep, _ = own_maxima.shape
    per = LANES // (candidates.shape[0] * query_len)
    total = n * deep * per
    vmem = pl.BlockSpec(memory_space=pltpu.VMEM)
    return pl.pallas_call(
        functools.partial(assemble_kernel, query_len),
        out_shape=jax.ShapeDtypeStruct(candidates.shape, jnp.float32),
        in_specs=[vmem] * 4,
        out_specs=vmem,
        scratch_shapes=[pltpu.VMEM((total + 8, LANES), jnp.float32)],
        compiler_params=pltpu.CompilerParams(vmem_limit_bytes=GRANT),
        name="assemble",
    )(own_maxima, more, starts, candidates)


def per_device(
    queries,
    candidates,
    centroids,
    bucket_weights,
    centroid_shard,
    centroid_row,
    residual_codes,
    tile_count,
    last_fill,
):
    n = lax.axis_size("psg")
    place = lax.axis_index("psg").astype(jnp.int32).reshape(1)
    num_queries, query_len, dim = queries.shape
    tiles_dev = residual_codes.shape[0] // TILE
    counts, lasts = in_blocks(tile_count), in_blocks(last_fill)
    codes = centroid_shard[:, 0] * centroids.shape[0] + centroid_row
    residual = jnp.where(
        residual_codes < 2,
        jnp.where(residual_codes == 0, bucket_weights[0], bucket_weights[1]),
        jnp.where(residual_codes == 2, bucket_weights[2], bucket_weights[3]),
    )
    fill = own_fill(place, counts, lasts, tiles_dev)
    query_rows = num_queries * query_len
    own = jnp.concatenate([centroids, queries.reshape(query_rows, dim)])
    held, (codes, fill, counts, residual) = spread(own, (codes, fill, counts, residual))
    maxima = tile_maxima(held, place, codes, fill, residual, query_rows)
    maxima, counts = lax.optimization_barrier((maxima, counts))
    starts, more = tile_starts(counts, tiles_dev * n)
    own_maxima = lax.all_to_all(maxima, "psg", split_axis=0, concat_axis=0, tiled=True)
    return assemble(own_maxima, more, starts, candidates, query_len)


def solution(mesh):
    placed = (
        P(("groups", "psg"), None, None),
        P(("groups", "psg"), None),
        P("psg", None),
        P(),
        P("psg", None),
        P("psg"),
        P("psg", None),
        P(),
        P(),
    )
    return jax.shard_map(
        per_device,
        mesh=mesh,
        in_specs=placed,
        out_specs=P(("groups", "psg"), None),
        check_vma=False,
    )
```

```python
import functools

import jax
import jax.numpy as jnp
from jax import lax
from jax.experimental import pallas as pl
from jax.experimental.pallas import tpu as pltpu
from jax.sharding import PartitionSpec as P


TILE = 128
LANES = 128
EPSILON = 1e-06
GRANT = 8 << 20


def swap(x, offset):
    n = lax.axis_size("psg")
    return lax.ppermute(x, "psg", [(i, i ^ offset) for i in range(n)])


def bits_of(n):
    return [1 << k for k in reversed(range(n.bit_length() - 1))]


def flipped(n):
    return n - n // 4


def spread(book, queries, beside):
    bits = bits_of(lax.axis_size("psg"))
    far, mid, low = bits[:3]
    half = book.shape[0] // 2
    far_book, far_queries = swap(book, far), swap(queries, far)
    own = jnp.concatenate([book, queries])
    taken = lax.dynamic_slice_in_dim(own, lax.axis_index("groups") * half, half, 0)
    some = jnp.concatenate([taken, queries])
    held = {(0, 0): own}
    held[low, 0] = swap(own, low)
    held[mid ^ low, 1] = swap(some, mid ^ low)
    held[mid, 1] = swap(some, mid)
    held[far, 0] = jnp.concatenate([far_book, far_queries])
    for offset in (low, mid ^ low, mid):
        held[far ^ offset, 0] = swap(held[far, 0], offset)
    for offset in (mid ^ low, mid):
        held[offset, 2] = lax.ppermute(held[offset, 1][:half], "groups", [(0, 1), (1, 0)])
    held[far ^ low, 0], beside = lax.optimization_barrier((held[far ^ low, 0], beside))
    pieces = [((segment,), array) for segment, array in held.items()]
    for bit in bits[3:]:
        if len(pieces) > 10:
            pieces = [(sum([names for names, _ in pieces], ()), jnp.concatenate([a for _, a in pieces]))]
        pieces = pieces + [(tuple((o ^ bit, part) for o, part in names), swap(array, bit)) for names, array in pieces]
    return pieces, beside


def passages(count_ref):
    count = count_ref[...]
    before = lax.broadcasted_iota(jnp.int32, (LANES, LANES), 0) < lax.broadcasted_iota(jnp.int32, (LANES, LANES), 1)
    within = jnp.dot(
        count.astype(jnp.float32).astype(jnp.bfloat16),
        jnp.where(before, 1.0, 0.0).astype(jnp.bfloat16),
        preferred_element_type=jnp.float32,
    ).astype(jnp.int32)
    sums = jnp.sum(count, axis=1, keepdims=True)
    passed = jnp.zeros((1, 1), jnp.int32)
    spans = []
    for b in range(count.shape[0]):
        held = count[b : b + 1, :]
        start = within[b : b + 1, :] + passed
        passed = passed + sums[b : b + 1, :]
        spans.append((start, jnp.where(held > 0, start + held - 1, -1)))
    return spans


def fill_kernel(place_ref, count_ref, last_ref, fill_ref):
    rows = fill_ref.shape[0]
    tile = lax.broadcasted_iota(jnp.int32, (rows, LANES), 0) + place_ref[0] * rows
    total = jnp.zeros((rows, LANES), jnp.int32)
    for b, (_, last) in enumerate(passages(count_ref)):
        total = total + jnp.where(tile == last, last_ref[b : b + 1, :] - TILE, 0)
    fill_ref[...] = jnp.broadcast_to(jnp.sum(total, axis=1, keepdims=True), (rows, LANES)) + TILE


def start_kernel(count_ref, start_ref, more_ref):
    spans = passages(count_ref)
    for b, (start, _) in enumerate(spans):
        start_ref[b : b + 1, :] = start

    def chunk(step, carry):
        first = pl.multiple_of(step * LANES, LANES)
        tile = lax.broadcasted_iota(jnp.int32, (LANES, LANES), 0) + first
        total = jnp.zeros((LANES, LANES), jnp.int32)
        for start, last in spans:
            total = total + jnp.where((start <= tile) & (tile <= last), last - tile, 0)
        more_ref[pl.ds(first, LANES), :] = jnp.broadcast_to(jnp.sum(total, axis=1, keepdims=True), (LANES, LANES))
        return carry

    lax.fori_loop(0, more_ref.shape[0] // LANES, chunk, 0)


def in_blocks(values):
    blocks = -(-values.shape[0] // LANES)
    return jnp.pad(values, (0, blocks * LANES - values.shape[0])).reshape(blocks, LANES)


def own_fill(place, counts, lasts, tiles_dev):
    vmem = pl.BlockSpec(memory_space=pltpu.VMEM)
    return pl.pallas_call(
        fill_kernel,
        out_shape=jax.ShapeDtypeStruct((tiles_dev, LANES), jnp.int32),
        in_specs=[pl.BlockSpec(memory_space=pltpu.SMEM), vmem, vmem],
        out_specs=vmem,
        compiler_params=pltpu.CompilerParams(vmem_limit_bytes=GRANT),
        name="own_fill",
    )(place, counts, lasts)


def tile_starts(counts, total_tiles):
    vmem = pl.BlockSpec(memory_space=pltpu.VMEM)
    return pl.pallas_call(
        start_kernel,
        out_shape=(
            jax.ShapeDtypeStruct(counts.shape, jnp.int32),
            jax.ShapeDtypeStruct((-(-total_tiles // LANES) * LANES, LANES), jnp.int32),
        ),
        in_specs=[vmem],
        out_specs=(vmem, vmem),
        compiler_params=pltpu.CompilerParams(vmem_limit_bytes=GRANT),
        name="tile_starts",
    )(counts)


def maxima_kernel(segments, place_ref, code_ref, fill_ref, residual_ref, *rest):
    pieces = rest[: len(segments)]
    out_ref, book_ref, query_ref, picked_ref, near_ref, rear_ref, best_ref = rest[len(segments) :]
    index = place_ref[0]
    peers = out_ref.shape[0]
    query_rows = query_ref.shape[0] // peers
    cent_dev = book_ref.shape[0] // peers
    group = place_ref[1]
    for names, piece in zip(segments, pieces):
        start = 0
        for offset, part in names:
            source = index ^ offset
            rows = cent_dev // (2 if part else 1)
            book_at = source * cent_dev
            if part:
                book_at = book_at + (group if part == 1 else 1 - group) * rows
            book_at = pl.multiple_of(book_at, LANES)

            def expand(step, carry, piece=piece, start=start, book_at=book_at):
                at = pl.multiple_of(step * LANES, LANES)
                values = piece[pl.ds(start + at, LANES), :].astype(jnp.float32)
                book_ref[pl.ds(book_at + at, LANES), :] = values
                return carry

            lax.fori_loop(0, rows // LANES, expand, 0, unroll=len(segments) > 8)
            start = start + rows
            if part < 2:
                query_at = pl.multiple_of(source * query_rows, query_rows)
                query_ref[pl.ds(query_at, query_rows), :] = piece[start : start + query_rows, :]
                start = start + query_rows

    tiles = residual_ref.shape[0] // TILE
    half = tiles // 2
    slot = lax.broadcasted_iota(jnp.int32, (TILE, LANES), 0)

    def pick(first, count):
        for u in range(first, first + count):
            picked_ref[u : u + 1, :] = book_ref[pl.ds(code_ref[u], 1), :]

    def decode(tile, into, first):
        summed = picked_ref[tile * TILE : (tile + 1) * TILE, :] + residual_ref[tile * TILE : (tile + 1) * TILE, :]
        scale = lax.rsqrt(jnp.sum(summed * summed, axis=1, keepdims=True) + EPSILON)
        embedded = summed * scale
        embedded = jnp.where(slot < fill_ref[tile : tile + 1, :], embedded, embedded[0:1, :])
        into[(tile - first) * TILE : (tile - first + 1) * TILE, :] = embedded.astype(jnp.bfloat16)

    def maxima(embedded, step, between=None):
        q = query_ref[pl.ds(pl.multiple_of(step * width, width), width), :]
        found = []
        for t in range(half):
            products = lax.dot_general(
                embedded[t * TILE : (t + 1) * TILE, :],
                q,
                (((1,), (1,)), ((), ())),
                preferred_element_type=jnp.float32,
            )
            found.append(jnp.max(products, axis=0, keepdims=True))
            if between is not None:
                between(t)
        return jnp.concatenate(found, axis=0)

    width = 2 * LANES
    steps = query_ref.shape[0] // width
    for tile in range(half):
        pick(tile * TILE, TILE)
        if tile:
            decode(tile - 1, near_ref, 0)
    pick(half * TILE, TILE)
    decode(half - 1, near_ref, 0)

    def beside(t, step):
        done = (half + 1) * TILE + (step * half + t) * part
        count = min(part, tiles * TILE - done)
        if count <= 0:
            return
        pick(done, count)
        if (done + count) % TILE == 0:
            decode((done + count) // TILE - 2, rear_ref, half)

    part = -(-(half - 1) * TILE // (min(steps, half // 2) * half) // 8) * 8
    for step in range(steps):
        best_ref[step] = maxima(near_ref, step, functools.partial(beside, step=step))
    decode(tiles - 1, rear_ref, half)

    lane = lax.broadcasted_iota(jnp.int32, (half, LANES), 1)

    def late(step, carry):
        first = best_ref[step]
        second = maxima(rear_ref, step)
        for b in range(width // LANES):
            one = first[:, b * LANES : (b + 1) * LANES]
            two = second[:, b * LANES : (b + 1) * LANES]
            peer = step * (width // query_rows) + 2 * b
            out_ref[peer ^ flipped(peers)] = jnp.where(lane < query_rows, one, pltpu.roll(two, query_rows, 1))
            out_ref[(peer + 1) ^ flipped(peers)] = jnp.where(lane < query_rows, pltpu.roll(one, query_rows, 1), two)
        return carry

    lax.fori_loop(0, steps, late, 0)


def tile_maxima(held, place, codes, fill, residual, cent_dev, query_rows):
    n = lax.axis_size("psg")
    tokens, dim = residual.shape
    tiles = tokens // TILE
    width = 2 * LANES
    if lax.axis_size("groups") != 2 or cent_dev % (2 * LANES) or 2 * query_rows != LANES or tiles % 4 or n * query_rows % width:
        raise ValueError("unsupported sizes")
    smem = pl.BlockSpec(memory_space=pltpu.SMEM)
    vmem = pl.BlockSpec(memory_space=pltpu.VMEM)
    room = (n * (cent_dev * 6 + query_rows * 4) + tokens * 10) * dim + GRANT
    return pl.pallas_call(
        functools.partial(maxima_kernel, tuple(o for o, _ in held)),
        out_shape=jax.ShapeDtypeStruct((n, tiles // 2, LANES), jnp.float32),
        in_specs=[smem, smem, vmem, vmem] + [vmem] * len(held),
        out_specs=vmem,
        scratch_shapes=[
            pltpu.VMEM((n * cent_dev, dim), jnp.float32),
            pltpu.VMEM((n * query_rows, dim), jnp.bfloat16),
            pltpu.VMEM((tokens, dim), jnp.float32),
            pltpu.VMEM((tokens // 2, dim), jnp.bfloat16),
            pltpu.VMEM((tokens // 2, dim), jnp.bfloat16),
            pltpu.VMEM((n * query_rows // width, tiles // 2, width), jnp.float32),
        ],
        compiler_params=pltpu.CompilerParams(vmem_limit_bytes=room),
        name="tile_maxima",
    )(place, codes, fill, residual, *[a for _, a in held])


def lookup(table, rows_of):
    within = rows_of & (LANES - 1)
    block = rows_of >> 7
    found = None
    for b, values in enumerate(table):
        got = jnp.take_along_axis(values, within, axis=1, mode="promise_in_bounds")
        found = got if found is None else jnp.where(block == b, got, found)
    return found


def assemble_kernel(query_len, maxima_ref, more_ref, start_ref, candidate_ref, out_ref, tiles_ref):
    n, deep, _ = maxima_ref.shape
    queries, candidates = candidate_ref.shape
    query_rows = queries * query_len
    per = LANES // query_rows
    total = n * deep * per
    for j in range(n):
        got = maxima_ref[j ^ flipped(n)]
        for g in range(per):
            at = (j * per + g) * deep
            part = got if g == 0 else pltpu.roll(got, LANES - g * query_rows, 1)
            tiles_ref[at : at + deep, :] = part
    tiles_ref[total : total + 8, :] = jnp.zeros((8, LANES), jnp.float32)
    more = more_ref[0:total, :]
    combined = tiles_ref[0:total, :]
    combined = jnp.maximum(combined, jnp.where(more >= 1, tiles_ref[1 : total + 1, :], combined))
    combined = jnp.maximum(combined, jnp.where(more >= 2, tiles_ref[2 : total + 2, :], combined))
    chunks = candidates // LANES
    row = lax.broadcasted_iota(jnp.int32, (8, LANES), 0)
    lane = lax.broadcasted_iota(jnp.int32, (8, LANES), 1)
    high = combined.astype(jnp.bfloat16)
    left = combined - high.astype(jnp.float32)
    middle = left.astype(jnp.bfloat16)
    low = (left - middle.astype(jnp.float32)).astype(jnp.bfloat16)
    groups = [(q, c) for q in range(queries) for c in range(chunks)]
    for first in range(0, len(groups), 8):
        some = groups[first : first + 8]
        owner = jnp.zeros((8, LANES), jnp.int32)
        wanted = jnp.zeros((8, LANES), jnp.int32)
        for r, (q, c) in enumerate(some):
            owner = jnp.where(row == r, q, owner)
            ids = candidate_ref[q : q + 1, c * LANES : (c + 1) * LANES]
            wanted = jnp.where(row == r, ids, wanted)
        select = jnp.where((lane >= owner * query_len) & (lane < (owner + 1) * query_len), 1.0, 0.0).astype(jnp.bfloat16)
        sums = None
        for part in (low, middle, high):
            term = lax.dot_general(select, part, (((1,), (1,)), ((), ())), preferred_element_type=jnp.float32)
            sums = term if sums is None else sums + term
        starts = [
            jnp.broadcast_to(start_ref[b : b + 1, :], (8, LANES)) for b in range(start_ref.shape[0])
        ]
        first_tile = lookup(starts, wanted)
        found = lookup([sums[:, b * LANES : (b + 1) * LANES] for b in range(-(-total // LANES))], first_tile)
        for r, (q, c) in enumerate(some):
            out_ref[q : q + 1, c * LANES : (c + 1) * LANES] = found[r : r + 1, :]


def assemble(own_maxima, more, starts, candidates, query_len):
    n, deep, _ = own_maxima.shape
    per = LANES // (candidates.shape[0] * query_len)
    total = n * deep * per
    vmem = pl.BlockSpec(memory_space=pltpu.VMEM)
    return pl.pallas_call(
        functools.partial(assemble_kernel, query_len),
        out_shape=jax.ShapeDtypeStruct(candidates.shape, jnp.float32),
        in_specs=[vmem] * 4,
        out_specs=vmem,
        scratch_shapes=[pltpu.VMEM((total + 8, LANES), jnp.float32)],
        compiler_params=pltpu.CompilerParams(vmem_limit_bytes=GRANT),
        name="assemble",
    )(own_maxima, more, starts, candidates)


def per_device(
    queries,
    candidates,
    centroids,
    bucket_weights,
    centroid_shard,
    centroid_row,
    residual_codes,
    tile_count,
    last_fill,
):
    n = lax.axis_size("psg")
    place = jnp.stack([lax.axis_index("psg"), lax.axis_index("groups")]).astype(jnp.int32)
    num_queries, query_len, dim = queries.shape
    tiles_dev = residual_codes.shape[0] // TILE
    counts, lasts = in_blocks(tile_count), in_blocks(last_fill)
    codes = centroid_shard[:, 0] * centroids.shape[0] + centroid_row
    residual = jnp.where(
        residual_codes < 2,
        jnp.where(residual_codes == 0, bucket_weights[0], bucket_weights[1]),
        jnp.where(residual_codes == 2, bucket_weights[2], bucket_weights[3]),
    )
    fill = own_fill(place, counts, lasts, tiles_dev)
    query_rows = num_queries * query_len
    held, (codes, fill, counts, residual) = spread(
        centroids, queries.reshape(query_rows, dim), (codes, fill, counts, residual)
    )
    maxima = tile_maxima(held, place, codes, fill, residual, centroids.shape[0], query_rows)
    maxima, counts = lax.optimization_barrier((maxima, counts))
    starts, more = tile_starts(counts, tiles_dev * n)
    own_maxima = lax.all_to_all(
        maxima, "psg", split_axis=0, concat_axis=0, tiled=True, axis_index_groups=[[k ^ flipped(n) for k in range(n)]]
    )
    return assemble(own_maxima, more, starts, candidates, query_len)


def solution(mesh):
    placed = (
        P(("groups", "psg"), None, None),
        P(("groups", "psg"), None),
        P("psg", None),
        P(),
        P("psg", None),
        P("psg"),
        P("psg", None),
        P(),
        P(),
    )
    return jax.shard_map(
        per_device,
        mesh=mesh,
        in_specs=placed,
        out_specs=P(("groups", "psg"), None),
        check_vma=False,
    )
```

```python
import functools

import jax
import jax.numpy as jnp
from jax import lax
from jax.experimental import pallas as pl
from jax.experimental.pallas import tpu as pltpu
from jax.sharding import PartitionSpec as P


TILE = 128
LANES = 128
EPSILON = 1e-06
GRANT = 8 << 20


def swap(x, offset):
    n = lax.axis_size("psg")
    return lax.ppermute(x, "psg", [(i, i ^ offset) for i in range(n)])


def bits_of(n):
    return [1 << k for k in reversed(range(n.bit_length() - 1))]


def flipped(n):
    return (n - n // 4) | 1


def spread(book, queries, beside):
    bits = bits_of(lax.axis_size("psg"))
    far, mid, low = bits[:3]
    half = book.shape[0] // 2
    far_book, far_queries = swap(book, far), swap(queries, far)
    own = jnp.concatenate([book, queries])
    taken = lax.dynamic_slice_in_dim(own, lax.axis_index("groups") * half, half, 0)
    some = jnp.concatenate([taken, queries])
    held = {(0, 0): own}
    held[low, 0] = swap(own, low)
    held[mid ^ low, 1] = swap(some, mid ^ low)
    held[mid, 1] = swap(some, mid)
    held[far, 0] = jnp.concatenate([far_book, far_queries])
    for offset in (low, mid ^ low, mid):
        held[far ^ offset, 0] = swap(held[far, 0], offset)
    for offset in (mid ^ low, mid):
        held[offset, 2] = lax.ppermute(held[offset, 1][:half], "groups", [(0, 1), (1, 0)])
    held[far ^ low, 0], beside = lax.optimization_barrier((held[far ^ low, 0], beside))
    pieces = [((segment,), array) for segment, array in held.items()]
    for bit in bits[3:]:
        if len(pieces) > 10:
            pieces = [(sum([names for names, _ in pieces], ()), jnp.concatenate([a for _, a in pieces]))]
        pieces = pieces + [(tuple((o ^ bit, part) for o, part in names), swap(array, bit)) for names, array in pieces]
    return pieces, beside


def passages(count_ref):
    count = count_ref[...]
    before = lax.broadcasted_iota(jnp.int32, (LANES, LANES), 0) < lax.broadcasted_iota(jnp.int32, (LANES, LANES), 1)
    within = jnp.dot(
        count.astype(jnp.float32).astype(jnp.bfloat16),
        jnp.where(before, 1.0, 0.0).astype(jnp.bfloat16),
        preferred_element_type=jnp.float32,
    ).astype(jnp.int32)
    sums = jnp.sum(count, axis=1, keepdims=True)
    passed = jnp.zeros((1, 1), jnp.int32)
    spans = []
    for b in range(count.shape[0]):
        held = count[b : b + 1, :]
        start = within[b : b + 1, :] + passed
        passed = passed + sums[b : b + 1, :]
        spans.append((start, jnp.where(held > 0, start + held - 1, -1)))
    return spans


def fill_kernel(place_ref, count_ref, last_ref, fill_ref):
    rows = fill_ref.shape[0]
    tile = lax.broadcasted_iota(jnp.int32, (rows, LANES), 0) + place_ref[0] * rows
    total = jnp.zeros((rows, LANES), jnp.int32)
    for b, (_, last) in enumerate(passages(count_ref)):
        total = total + jnp.where(tile == last, last_ref[b : b + 1, :] - TILE, 0)
    fill_ref[...] = jnp.broadcast_to(jnp.sum(total, axis=1, keepdims=True), (rows, LANES)) + TILE


def start_kernel(count_ref, start_ref, more_ref):
    spans = passages(count_ref)
    for b, (start, _) in enumerate(spans):
        start_ref[b : b + 1, :] = start

    def chunk(step, carry):
        first = pl.multiple_of(step * LANES, LANES)
        tile = lax.broadcasted_iota(jnp.int32, (LANES, LANES), 0) + first
        total = jnp.zeros((LANES, LANES), jnp.int32)
        for start, last in spans:
            total = total + jnp.where((start <= tile) & (tile <= last), last - tile, 0)
        more_ref[pl.ds(first, LANES), :] = jnp.broadcast_to(jnp.sum(total, axis=1, keepdims=True), (LANES, LANES))
        return carry

    lax.fori_loop(0, more_ref.shape[0] // LANES, chunk, 0)


def in_blocks(values):
    blocks = -(-values.shape[0] // LANES)
    return jnp.pad(values, (0, blocks * LANES - values.shape[0])).reshape(blocks, LANES)


def own_fill(place, counts, lasts, tiles_dev):
    vmem = pl.BlockSpec(memory_space=pltpu.VMEM)
    return pl.pallas_call(
        fill_kernel,
        out_shape=jax.ShapeDtypeStruct((tiles_dev, LANES), jnp.int32),
        in_specs=[pl.BlockSpec(memory_space=pltpu.SMEM), vmem, vmem],
        out_specs=vmem,
        compiler_params=pltpu.CompilerParams(vmem_limit_bytes=GRANT),
        name="own_fill",
    )(place, counts, lasts)


def tile_starts(counts, total_tiles):
    vmem = pl.BlockSpec(memory_space=pltpu.VMEM)
    return pl.pallas_call(
        start_kernel,
        out_shape=(
            jax.ShapeDtypeStruct(counts.shape, jnp.int32),
            jax.ShapeDtypeStruct((-(-total_tiles // LANES) * LANES, LANES), jnp.int32),
        ),
        in_specs=[vmem],
        out_specs=(vmem, vmem),
        compiler_params=pltpu.CompilerParams(vmem_limit_bytes=GRANT),
        name="tile_starts",
    )(counts)


def maxima_kernel(segments, place_ref, code_ref, fill_ref, residual_ref, *rest):
    pieces = rest[: len(segments)]
    out_ref, book_ref, query_ref, picked_ref, embedded_ref, best_ref = rest[len(segments) :]
    index = place_ref[0]
    peers = out_ref.shape[0]
    query_rows = query_ref.shape[0] // peers
    cent_dev = book_ref.shape[0] // peers
    group = place_ref[1]
    for names, piece in zip(segments, pieces):
        start = 0
        for offset, part in names:
            source = index ^ offset
            rows = cent_dev // (2 if part else 1)
            book_at = source * cent_dev
            if part:
                book_at = book_at + (group if part == 1 else 1 - group) * rows
            book_at = pl.multiple_of(book_at, LANES)

            def expand(step, carry, piece=piece, start=start, book_at=book_at):
                at = pl.multiple_of(step * LANES, LANES)
                values = piece[pl.ds(start + at, LANES), :].astype(jnp.float32)
                book_ref[pl.ds(book_at + at, LANES), :] = values
                return carry

            lax.fori_loop(0, rows // LANES, expand, 0, unroll=len(segments) > 8)
            start = start + rows
            if part < 2:
                query_at = pl.multiple_of(source * query_rows, query_rows)
                query_ref[pl.ds(query_at, query_rows), :] = piece[start : start + query_rows, :]
                start = start + query_rows

    tiles = residual_ref.shape[0] // TILE
    slot = lax.broadcasted_iota(jnp.int32, (TILE, LANES), 0)
    width = 2 * LANES
    steps = query_ref.shape[0] // width

    def pick(first, count):
        for u in range(first, first + count):
            picked_ref[u : u + 1, :] = book_ref[pl.ds(code_ref[u], 1), :]

    def decode(tile):
        rows = slice(tile * TILE, (tile + 1) * TILE)
        summed = picked_ref[rows, :] + residual_ref[rows, :]
        scale = lax.rsqrt(jnp.sum(summed * summed, axis=1, keepdims=True) + EPSILON)
        embedded = summed * scale
        embedded = jnp.where(slot < fill_ref[tile : tile + 1, :], embedded, embedded[0:1, :])
        embedded_ref[rows, :] = embedded.astype(jnp.bfloat16)

    def score(tile, step):
        products = lax.dot_general(
            embedded_ref[tile * TILE : (tile + 1) * TILE, :],
            query_ref[pl.ds(pl.multiple_of(step * width, width), width), :],
            (((1,), (1,)), ((), ())),
            preferred_element_type=jnp.float32,
        )
        best_ref[step, tile : tile + 1, :] = jnp.max(products, axis=0, keepdims=True)

    together = steps <= 8
    for tile in range(tiles + 2):
        if together and tile >= 2:
            for step in range(steps):
                score(tile - 2, step)
                if tile < tiles:
                    pick(tile * TILE + step * TILE // steps, TILE // steps)
        elif tile < tiles:
            pick(tile * TILE, TILE)
        if 1 <= tile <= tiles:
            decode(tile - 1)

    if not together:

        def scores(step, carry):
            for tile in range(tiles):
                score(tile, step)
            return carry

        lax.fori_loop(0, steps, scores, 0)

    deep = tiles // 2
    lane = lax.broadcasted_iota(jnp.int32, (deep, LANES), 1)

    def arrange(step, carry):
        for b in range(width // LANES):
            one = best_ref[step, 0:deep, b * LANES : (b + 1) * LANES]
            two = best_ref[step, deep:tiles, b * LANES : (b + 1) * LANES]
            peer = step * (width // query_rows) + 2 * b
            out_ref[peer ^ flipped(peers)] = jnp.where(lane < query_rows, one, pltpu.roll(two, query_rows, 1))
            out_ref[(peer + 1) ^ flipped(peers)] = jnp.where(lane < query_rows, pltpu.roll(one, query_rows, 1), two)
        return carry

    lax.fori_loop(0, steps, arrange, 0, unroll=together)


def tile_maxima(held, place, codes, fill, residual, cent_dev, query_rows):
    n = lax.axis_size("psg")
    tokens, dim = residual.shape
    tiles = tokens // TILE
    width = 2 * LANES
    if lax.axis_size("groups") != 2 or cent_dev % (2 * LANES) or 2 * query_rows != LANES or tiles % 4 or n * query_rows % width:
        raise ValueError("unsupported sizes")
    smem = pl.BlockSpec(memory_space=pltpu.SMEM)
    vmem = pl.BlockSpec(memory_space=pltpu.VMEM)
    room = (n * (cent_dev * 6 + query_rows * 4) + tokens * 10) * dim + GRANT
    return pl.pallas_call(
        functools.partial(maxima_kernel, tuple(o for o, _ in held)),
        out_shape=jax.ShapeDtypeStruct((n, tiles // 2, LANES), jnp.float32),
        in_specs=[smem, smem, vmem, vmem] + [vmem] * len(held),
        out_specs=vmem,
        scratch_shapes=[
            pltpu.VMEM((n * cent_dev, dim), jnp.float32),
            pltpu.VMEM((n * query_rows, dim), jnp.bfloat16),
            pltpu.VMEM((tokens, dim), jnp.float32),
            pltpu.VMEM((tokens, dim), jnp.bfloat16),
            pltpu.VMEM((n * query_rows // width, tiles, width), jnp.float32),
        ],
        compiler_params=pltpu.CompilerParams(vmem_limit_bytes=room),
        name="tile_maxima",
    )(place, codes, fill, residual, *[a for _, a in held])


def lookup(table, rows_of):
    within = rows_of & (LANES - 1)
    block = rows_of >> 7
    found = None
    for b, values in enumerate(table):
        got = jnp.take_along_axis(values, within, axis=1, mode="promise_in_bounds")
        found = got if found is None else jnp.where(block == b, got, found)
    return found


def assemble_kernel(query_len, maxima_ref, more_ref, start_ref, candidate_ref, out_ref, tiles_ref):
    n, deep, _ = maxima_ref.shape
    queries, candidates = candidate_ref.shape
    query_rows = queries * query_len
    per = LANES // query_rows
    total = n * deep * per
    for j in range(n):
        got = maxima_ref[j ^ flipped(n)]
        for g in range(per):
            at = (j * per + g) * deep
            part = got if g == 0 else pltpu.roll(got, LANES - g * query_rows, 1)
            tiles_ref[at : at + deep, :] = part
    tiles_ref[total : total + 8, :] = jnp.zeros((8, LANES), jnp.float32)
    more = more_ref[0:total, :]
    combined = tiles_ref[0:total, :]
    combined = jnp.maximum(combined, jnp.where(more >= 1, tiles_ref[1 : total + 1, :], combined))
    combined = jnp.maximum(combined, jnp.where(more >= 2, tiles_ref[2 : total + 2, :], combined))
    chunks = candidates // LANES
    row = lax.broadcasted_iota(jnp.int32, (8, LANES), 0)
    lane = lax.broadcasted_iota(jnp.int32, (8, LANES), 1)
    high = combined.astype(jnp.bfloat16)
    left = combined - high.astype(jnp.float32)
    middle = left.astype(jnp.bfloat16)
    low = (left - middle.astype(jnp.float32)).astype(jnp.bfloat16)
    groups = [(q, c) for q in range(queries) for c in range(chunks)]
    for first in range(0, len(groups), 8):
        some = groups[first : first + 8]
        owner = jnp.zeros((8, LANES), jnp.int32)
        wanted = jnp.zeros((8, LANES), jnp.int32)
        for r, (q, c) in enumerate(some):
            owner = jnp.where(row == r, q, owner)
            ids = candidate_ref[q : q + 1, c * LANES : (c + 1) * LANES]
            wanted = jnp.where(row == r, ids, wanted)
        select = jnp.where((lane >= owner * query_len) & (lane < (owner + 1) * query_len), 1.0, 0.0).astype(jnp.bfloat16)
        sums = None
        for part in (low, middle, high):
            term = lax.dot_general(select, part, (((1,), (1,)), ((), ())), preferred_element_type=jnp.float32)
            sums = term if sums is None else sums + term
        starts = [
            jnp.broadcast_to(start_ref[b : b + 1, :], (8, LANES)) for b in range(start_ref.shape[0])
        ]
        first_tile = lookup(starts, wanted)
        found = lookup([sums[:, b * LANES : (b + 1) * LANES] for b in range(-(-total // LANES))], first_tile)
        for r, (q, c) in enumerate(some):
            out_ref[q : q + 1, c * LANES : (c + 1) * LANES] = found[r : r + 1, :]


def assemble(own_maxima, more, starts, candidates, query_len):
    n, deep, _ = own_maxima.shape
    per = LANES // (candidates.shape[0] * query_len)
    total = n * deep * per
    vmem = pl.BlockSpec(memory_space=pltpu.VMEM)
    return pl.pallas_call(
        functools.partial(assemble_kernel, query_len),
        out_shape=jax.ShapeDtypeStruct(candidates.shape, jnp.float32),
        in_specs=[vmem] * 4,
        out_specs=vmem,
        scratch_shapes=[pltpu.VMEM((total + 8, LANES), jnp.float32)],
        compiler_params=pltpu.CompilerParams(vmem_limit_bytes=GRANT),
        name="assemble",
    )(own_maxima, more, starts, candidates)


def per_device(
    queries,
    candidates,
    centroids,
    bucket_weights,
    centroid_shard,
    centroid_row,
    residual_codes,
    tile_count,
    last_fill,
):
    n = lax.axis_size("psg")
    place = jnp.stack([lax.axis_index("psg"), lax.axis_index("groups")]).astype(jnp.int32)
    num_queries, query_len, dim = queries.shape
    tiles_dev = residual_codes.shape[0] // TILE
    counts, lasts = in_blocks(tile_count), in_blocks(last_fill)
    codes = centroid_shard[:, 0] * centroids.shape[0] + centroid_row
    residual = jnp.where(
        residual_codes < 2,
        jnp.where(residual_codes == 0, bucket_weights[0], bucket_weights[1]),
        jnp.where(residual_codes == 2, bucket_weights[2], bucket_weights[3]),
    )
    fill = own_fill(place, counts, lasts, tiles_dev)
    query_rows = num_queries * query_len
    held, (codes, fill, counts, residual) = spread(
        centroids, queries.reshape(query_rows, dim), (codes, fill, counts, residual)
    )
    maxima = tile_maxima(held, place, codes, fill, residual, centroids.shape[0], query_rows)
    maxima, counts = lax.optimization_barrier((maxima, counts))
    starts, more = tile_starts(counts, tiles_dev * n)
    own_maxima = lax.all_to_all(
        maxima, "psg", split_axis=0, concat_axis=0, tiled=True, axis_index_groups=[[k ^ flipped(n) for k in range(n)]]
    )
    return assemble(own_maxima, more, starts, candidates, query_len)


def solution(mesh):
    placed = (
        P(("groups", "psg"), None, None),
        P(("groups", "psg"), None),
        P("psg", None),
        P(),
        P("psg", None),
        P("psg"),
        P("psg", None),
        P(),
        P(),
    )
    return jax.shard_map(
        per_device,
        mesh=mesh,
        in_specs=placed,
        out_specs=P(("groups", "psg"), None),
        check_vma=False,
    )
```
